32 devices in a mesh: stn: 4 (over z), tm: 8 (over y, x, core).
Axes of the slice: x: 2, y: 2, z: 4, core: 2. Of those that a mesh axis runs over, the one named last changes fastest.
Arguments:
- voltages: bfloat16 [128, 2, 2, 256, 2048], P('tm', None, None, 'stn'), may hold values from -6 to 6
- taps: float32 [16, 2048], replicated, may hold values from -1.5 to 1.5
- sk_tolerance: float32 [384], P('tm'), may hold values from 0.05 to 0.3
- station_coords: int32 [256, 2], replicated, may hold values from 0 to 1023
- pointings: int32 [256, 2], replicated, may hold values from -64 to 64
- station_flags: int32 [256], replicated, may hold values 0 or 1
Outputs:
- beam_power: float32 [384, 8, 256], P('tm', None, 'stn')
The draws below stay inside these ranges and needn't reach their ends.
All inputs are finite; a program needn't handle non-finite values.
Results may differ from the reference program's by a relative error of at most 0.0045.
Values may be sent and summed in bfloat16 or wider, within the bound.
A program may use at most 128 MiB of HBM per device.

```python
import math
import jax
import jax.numpy as jnp
from jax import lax

F_DEV = 16
STATIONS = 256
NFFT = 2048
CHAN = 384
TAPS = 16
BEAMS = 256
INTEG = 16
S_DEV = 64
FRAMES = 128
N_STN = 4


def plant(drawn, stream_key, low, largest):
    longest = drawn.shape.index(max(drawn.shape))
    spots = []
    for shift in (0, 1):
        where = [jax.random.randint(jax.random.fold_in(stream_key, axis), (), 0, length) for axis, length in enumerate(drawn.shape)]
        where[longest] = (where[longest] + shift) % drawn.shape[longest]
        spots.append(tuple(where))
    return drawn.at[spots[0]].set(low).at[spots[1]].set(largest)


def shard_levels(stream_key, extent, split, least, high):
    factor_of = 1.0
    for dim, blocks in split:
        steps = jax.random.uniform(jax.random.fold_in(jax.random.fold_in(stream_key, 6), dim), (blocks,), jnp.float32, least / len(split), high / len(split))
        factor_of = factor_of * jnp.repeat(jnp.exp(steps), extent[dim] // blocks).reshape((-1,) + (1,) * (len(extent) - 1 - dim))
    return factor_of


def bell_draw(own_key, extent, scale, most, pieces=(), kind=jnp.bfloat16):
    array = scale * jax.random.normal(own_key, extent, jnp.float32)
    if pieces:
        array = array * shard_levels(own_key, extent, pieces, -0.22, 0.18)
    return jnp.clip(array, -most, most).astype(kind)


def setup_inputs(seed: int = 0) -> dict:
    streams_of = jax.random.split(jax.random.key(seed), 7)
    voltages = bell_draw(streams_of[0], (FRAMES, 2, 2, STATIONS, NFFT), 1.0, 6.0, ((0, 8), (3, 4)))
    taps = bell_draw(streams_of[1], (TAPS, NFFT), TAPS ** -0.5, 1.5, (), jnp.float32)
    sk_tolerance = jnp.clip(jnp.exp(math.log(0.3) - 1.7917595 * jax.random.uniform(streams_of[2], (CHAN,), jnp.float32) ** shard_levels(streams_of[2], (CHAN,), ((0, 8),), -0.2, 0.2)), 0.05, 0.3)
    station_coords = plant(jax.random.randint(streams_of[3], (STATIONS, 2), 0, 1024), jax.random.fold_in(streams_of[3], 1), 0, 1023).astype(jnp.int32)
    pointings = plant(jax.random.randint(streams_of[4], (BEAMS, 2), -64, 65), jax.random.fold_in(streams_of[4], 1), -64, 64).astype(jnp.int32)
    station_flags = plant((jax.random.randint(streams_of[5], (STATIONS,), 0, 8) < 1).astype(jnp.int32), jax.random.fold_in(streams_of[5], 1), 0, 1)
    return {"voltages": voltages, "taps": taps, "sk_tolerance": sk_tolerance, "station_coords": station_coords, "pointings": pointings, "station_flags": station_flags}


def fourier_table(channels, points):
    rows = jnp.arange(channels, dtype=jnp.int32)
    columns = jnp.arange(points, dtype=jnp.int32)
    residue = rows[:, None] * columns[None, :] % points
    angle = 2.0 * math.pi / points * residue.astype(jnp.float32)
    factor = 1.0 / math.sqrt(points)
    return jnp.concatenate([jnp.cos(angle) * factor, jnp.sin(angle) * factor], 0).astype(jnp.bfloat16)

def steering(channel_ids, coords, flags, pointings, scale):
    offsets = coords[:, 0:1] * pointings[None, :, 0] + coords[:, 1:2] * pointings[None, :, 1]
    residue = (channel_ids + 1)[:, None, None] * offsets[None, :, :] % 65536
    angle = 2.0 * math.pi / 65536.0 * residue.astype(jnp.float32)
    live_gain = (1 - flags).astype(jnp.float32) * scale
    real_part = (jnp.cos(angle) * live_gain[None, :, None]).astype(jnp.bfloat16)
    imag_part = (jnp.sin(angle) * live_gain[None, :, None]).astype(jnp.bfloat16)
    upper = jnp.concatenate([real_part, imag_part], 2)
    lower = jnp.concatenate([-imag_part, real_part], 2)
    return jnp.stack([upper, lower], 1)

def own_sum(block, taps):
    frames = block.shape[0]
    span = taps.shape[0] - 1
    padded = jnp.pad(block, ((span, 0), (0, 0), (0, 0), (0, 0), (0, 0)))
    return sum((padded[span - tap_index:span - tap_index + frames].astype(jnp.float32) * taps[tap_index] for tap_index in range(taps.shape[0])))

def carried_sum(last_frames, taps):
    span = taps.shape[0] - 1
    padded = jnp.pad(last_frames, ((0, span), (0, 0), (0, 0), (0, 0), (0, 0)))
    return sum((padded[span - tap_index:2 * span - tap_index].astype(jnp.float32) * taps[tap_index] for tap_index in range(1, span + 1)))

def transform(filtered, table):
    frames = filtered.shape[0]
    local = filtered.shape[3]
    points = filtered.shape[-1]
    flat = filtered.reshape(-1, points)
    product = lax.dot_general(table, flat, (((1,), (1,)), ((), ())), preferred_element_type=jnp.float32)
    channels = table.shape[0] // 2
    product = product.reshape(2, channels, frames, 2, 2, local)
    real_out = product[0, :, :, 0] + product[1, :, :, 1]
    imag_out = product[0, :, :, 1] - product[1, :, :, 0]
    return jnp.stack([real_out, imag_out], 3)

def channelize(block, taps, table):
    span = taps.shape[0] - 1
    last_frames = block[:span]
    own_block = block[span:]
    own_part = transform(own_sum(own_block, taps).astype(jnp.bfloat16), table)
    carried_part = transform(carried_sum(last_frames, taps).astype(jnp.bfloat16), table)
    leading = own_part[:, :span] + carried_part
    return jnp.concatenate([leading, own_part[:, span:]], 1).astype(jnp.bfloat16)

def soft_weights(spectra, tolerance):
    count, frames, polars, parts, local = spectra.shape
    half = frames // 2
    values = spectra.astype(jnp.float32).reshape(count, 2, half, polars, parts, local)
    power = lax.optimization_barrier(jnp.sum(values * values, 4))
    first_sum = lax.optimization_barrier(jnp.sum(power, 2))
    second_sum = lax.optimization_barrier(jnp.sum(power * power, 2))
    size = float(half)
    kurtosis = (size + 1.0) / (size - 1.0) * (size * second_sum / (first_sum * first_sum) - 1.0)
    deviation = (kurtosis - 1.0) / tolerance[:, None, None, None]
    soft = 1.0 / (1.0 + deviation * deviation)
    weighted = values * soft[:, :, None, :, None, :]
    return weighted.astype(jnp.bfloat16).reshape(count, frames, polars, parts, local)

def reference(voltages, taps, sk_tolerance, station_coords, pointings, station_flags):
    frames_all = voltages.shape[0]
    span = TAPS - 1
    table = fourier_table(CHAN, NFFT)
    scale = 1.0 / math.sqrt(STATIONS)

    def one_block(index):
        own = lax.dynamic_slice_in_dim(voltages, index * F_DEV, F_DEV, 0)
        back = jnp.maximum(index * F_DEV - span, 0).astype(jnp.int32)
        prior = lax.dynamic_slice_in_dim(voltages, back, span, 0)
        prior = jnp.where(index > 0, prior, jnp.zeros_like(prior))
        return channelize(jnp.concatenate([prior, own], 0), taps, table)
    spectra = lax.map(one_block, jnp.arange(frames_all // F_DEV, dtype=jnp.int32))
    spectra = jnp.moveaxis(spectra, 0, 1).reshape(CHAN, frames_all, 2, 2, STATIONS)

    def one_channel(inputs):
        channel, values, tolerance = inputs
        weighted = soft_weights(values[None], tolerance[None])[0]
        weights = steering(channel[None], station_coords, station_flags, pointings, scale)[0]
        grouped = weighted.astype(jnp.float32).reshape(frames_all, 2, 2, N_STN, S_DEV)
        weight_groups = weights.astype(jnp.float32).reshape(2, N_STN, S_DEV, 2 * BEAMS)
        partial_value = jnp.einsum('tprgs,rgsj->gtpj', grouped, weight_groups)
        partial_value = lax.optimization_barrier(partial_value.astype(jnp.bfloat16)).astype(jnp.float32)
        beam = lax.optimization_barrier(jnp.sum(partial_value, 0))
        squares = (beam * beam).reshape(frames_all // INTEG, INTEG, 2, 2, BEAMS)
        return lax.optimization_barrier(jnp.sum(squares, (1, 2, 3))) / (2.0 * INTEG)
    return lax.map(one_channel, (jnp.arange(CHAN, dtype=jnp.int32), spectra, sk_tolerance))
```

```python
import functools
import math

import jax
import jax.numpy as jnp
from jax import lax
from jax.experimental import pallas as pl
from jax.experimental.pallas import tpu as pltpu
from jax.sharding import PartitionSpec as P

INTEG = 16


def passed_along(block, axis, distance):
    devices = range(lax.axis_size(axis))
    route = [(i - distance, i) for i in devices if i - distance in devices]
    return lax.ppermute(block, axis, route)


def fourier_table(channels, points, chunk):
    rows = jnp.arange(channels, dtype=jnp.int32)
    columns = jnp.arange(points, dtype=jnp.int32)
    residue = rows[:, None] * columns[None, :] % points
    angle = 2.0 * math.pi / points * residue.astype(jnp.float32)
    factor = 1.0 / math.sqrt(points)
    cosine = (jnp.cos(angle) * factor).astype(jnp.bfloat16)
    sine = (jnp.sin(angle) * factor).astype(jnp.bfloat16)
    cosine = cosine.reshape(channels, points // chunk, chunk)
    sine = sine.reshape(channels, points // chunk, chunk)
    upper = jnp.concatenate([cosine, sine], 2)
    lower = jnp.concatenate([-sine, cosine], 2)
    return jnp.moveaxis(jnp.concatenate([upper, lower], 0), 1, 0)


def steering(channel_ids, coords, flags, pointings, scale):
    offsets = coords[:, 0:1] * pointings[None, :, 0] + coords[:, 1:2] * pointings[None, :, 1]
    residue = (channel_ids + 1)[:, None, None] * offsets[None, :, :] % 65536
    angle = 2.0 * math.pi / 65536.0 * residue.astype(jnp.float32)
    live_gain = (1 - flags).astype(jnp.float32) * scale
    real_part = (jnp.cos(angle) * live_gain[None, :, None]).astype(jnp.bfloat16)
    imag_part = (jnp.sin(angle) * live_gain[None, :, None]).astype(jnp.bfloat16)
    upper = jnp.concatenate([real_part, imag_part], 2)
    lower = jnp.concatenate([-imag_part, real_part], 2)
    return jnp.stack([upper, lower], 1)


def filter_kernel(volt_ref, taps_ref, table_ref, out_ref, x_ref, acc_ref, *, carried):
    frames, _, local, chunk = volt_ref.shape
    count = taps_ref.shape[0]
    step = pl.program_id(1)
    rows = 16
    lanes = 128
    lane_blocks = chunk // lanes
    row_blocks = local // rows

    def tile(index, unused):
        part = index // (lane_blocks * row_blocks)
        lane = pl.multiple_of(index // row_blocks % lane_blocks * lanes, lanes)
        row = pl.multiple_of(index % row_blocks * rows, rows)
        column = pl.multiple_of(part * chunk + lane, lanes)
        gains = [taps_ref[k : k + 1, pl.ds(lane, lanes)] for k in range(count)]
        values = [
            volt_ref[f, part, pl.ds(row, rows), pl.ds(lane, lanes)].astype(jnp.float32)
            for f in range(frames)
        ]
        for f in range(frames):
            total = jnp.zeros((rows, lanes), jnp.float32)
            for k in range(count):
                source = f - k + (frames if carried else 0)
                if 0 <= source < frames:
                    total = total + values[source] * gains[k]
            x_ref[pl.ds(f * local + row, rows), pl.ds(column, lanes)] = total.astype(jnp.bfloat16)
        return unused

    lax.fori_loop(0, 2 * lane_blocks * row_blocks, tile, 0)
    product = lax.dot_general(
        table_ref[...], x_ref[...], (((1,), (1,)), ((), ())), preferred_element_type=jnp.float32
    )

    @pl.when(step == 0)
    def _():
        acc_ref[...] = product

    @pl.when(step > 0)
    def _():
        acc_ref[...] = acc_ref[...] + product

    @pl.when(step == pl.num_programs(1) - 1)
    def _():
        out_ref[...] = acc_ref[...].astype(out_ref.dtype)


def filterbank(voltages, taps, table, carried, kind):
    frames, parts, polars, local, points = voltages.shape
    chunks, outs, width = table.shape
    chunk = width // parts
    return pl.pallas_call(
        functools.partial(filter_kernel, carried=carried),
        grid=(polars, chunks),
        in_specs=[
            pl.BlockSpec((frames, parts, None, local, chunk), lambda p, i: (0, 0, p, 0, i)),
            pl.BlockSpec((taps.shape[0], chunk), lambda p, i: (0, i)),
            pl.BlockSpec((None, outs, width), lambda p, i: (i, 0, 0)),
        ],
        out_specs=pl.BlockSpec((outs, frames * local), lambda p, i: (0, p)),
        out_shape=jax.ShapeDtypeStruct((outs, polars * frames * local), kind),
        scratch_shapes=[
            pltpu.VMEM((frames * local, width), jnp.bfloat16),
            pltpu.VMEM((outs, frames * local), jnp.float32),
        ],
        compiler_params=pltpu.CompilerParams(
            dimension_semantics=("arbitrary", "arbitrary"), vmem_limit_bytes=56 * 1024 * 1024
        ),
    )(voltages, taps, table)


def per_device(voltages, taps, sk_tolerance, station_coords, pointings, station_flags):
    frames, parts, polars, local, points = voltages.shape
    blocks = lax.axis_size("tm")
    groups = lax.axis_size("stn")
    owned = sk_tolerance.shape[0]
    channels = owned * blocks
    count = -(-owned // groups)
    spare = count * groups - owned
    beams = pointings.shape[0]
    table = fourier_table(channels, points, min(512, points))
    outgoing = filterbank(voltages, taps, table, True, jnp.bfloat16)
    received = passed_along(outgoing, "tm", 1)
    own_part = filterbank(voltages, taps, table, False, jnp.float32)
    spectra = (own_part + received.astype(jnp.float32)).astype(jnp.bfloat16)
    length = polars * frames * local
    spectra = jnp.swapaxes(spectra.reshape(2, channels, length), 0, 1)
    if spare:
        spectra = spectra.reshape(blocks, owned, 2, length)
        spectra = jnp.pad(spectra, ((0, 0), (0, spare), (0, 0), (0, 0)))
        spectra = spectra.reshape(blocks * (owned + spare), 2, length)
        sk_tolerance = jnp.pad(sk_tolerance, (0, spare), constant_values=1.0)
    turned = lax.all_to_all(spectra, ("tm", "stn"), split_axis=0, concat_axis=0, tiled=True)
    turned = turned.reshape(blocks, groups, count, 2, polars, frames, local)
    grouped = jnp.transpose(turned, (2, 4, 0, 5, 3, 1, 6))
    windows = 2
    size = float(blocks * frames // windows)
    shape = (count * polars, windows, blocks // windows, frames, 2, groups, local)
    values = grouped.reshape(shape).astype(jnp.float32)
    first = lax.axis_index("stn") * count
    tolerance = jnp.repeat(lax.dynamic_slice_in_dim(sk_tolerance, first, count, 0), polars)
    power = values * values
    power = power[:, :, :, :, 0] + power[:, :, :, :, 1]
    first_sum = jnp.sum(power, (2, 3))
    second_sum = jnp.sum(power * power, (2, 3))
    kurtosis = (size + 1.0) / (size - 1.0) * (size * second_sum / (first_sum * first_sum) - 1.0)
    deviation = (kurtosis - 1.0) / tolerance[:, None, None, None]
    soft = 1.0 / (1.0 + deviation * deviation)
    weighted = (values * soft[:, :, None, None, None]).astype(jnp.bfloat16)
    stations = groups * local
    weighted = weighted.reshape(count, polars * blocks * frames, 2 * stations)
    channel_ids = lax.axis_index("tm") * owned + first + jnp.arange(count, dtype=jnp.int32)
    scale = 1.0 / math.sqrt(stations)
    weights = steering(channel_ids, station_coords, station_flags, pointings, scale)
    weights = weights.reshape(count, 2 * stations, 2 * beams)
    beam = jnp.einsum("ctk,ckj->ctj", weighted, weights, preferred_element_type=jnp.float32)
    squares = beam * beam
    squares = squares[:, :, :beams] + squares[:, :, beams:]
    squares = squares.reshape(count, polars, blocks * frames // INTEG, INTEG, beams)
    result = jnp.sum(squares, (1, 3)) / (2.0 * INTEG)
    return lax.all_to_all(result, "stn", split_axis=2, concat_axis=0, tiled=True)[:owned]


def solution(mesh):
    in_specs = (P("tm", None, None, "stn", None), P(), P("tm"), P(), P(), P())
    out_specs = P("tm", None, "stn")
    return jax.shard_map(
        per_device, mesh=mesh, in_specs=in_specs, out_specs=out_specs, check_vma=False
    )
```
